256 devices in a mesh: rows: 16 (over z, core), cols: 16 (over y, x).
Axes of the slice: x: 4, y: 4, z: 8, core: 2. Of those that a mesh axis runs over, the one named last changes fastest.
Arguments:
- tensor: float32 [32, 2048, 2048], P(None, 'rows', 'cols'), may hold values from -819200 to 819200
- second_init: float32 [2048, 64], P('cols'), may hold values from -6 to 6
- third_init: float32 [32, 64], replicated, may hold values from -6 to 6
Outputs:
- first: float32 [2048, 64], P('rows')
- second: float32 [2048, 64], P('cols')
- third: float32 [32, 64], replicated
The draws below stay inside these ranges and needn't reach their ends.
All inputs are finite; a program needn't handle non-finite values.
Results may differ from the reference program's by a relative error of at most 0.0003.
Values sent between devices are 32-bit elements; how exact they have to be, the bound alone decides.
No kernel may reach another device: no remote copies, remote signals or barrier semaphores. Data moves between devices by JAX's collectives and lax.ppermute only.
A program may use at most 64 MiB of HBM per device.

```python
import jax
import jax.numpy as jnp
from jax import lax

K = 32
R = 64
ITERS = 5
I = 2048
J = 2048


def draw_tensor(key, part):
    key_noise = jax.random.fold_in(key, 11)
    key_rows = jax.random.fold_in(key, 12)
    key_cols = jax.random.fold_in(key, 13)
    key_time = jax.random.fold_in(key, 14)
    noise = jnp.clip(jax.random.normal(key_noise, (K, I, J), jnp.float32), -6.0, 6.0)
    spread = 10.0
    row_place = jnp.arange(I, dtype=jnp.float32) / I
    col_place = jnp.arange(J, dtype=jnp.float32) / J
    row_scale = jnp.power(3.0, row_place) * jnp.power(spread, jax.random.uniform(key_rows, (I,), jnp.float32))
    col_scale = jnp.power(3.0, col_place) * jnp.power(spread, jax.random.uniform(key_cols, (J,), jnp.float32))
    time_scale = jnp.power(2.0, jax.random.uniform(key_time, (K,), jnp.float32, -1.0, 1.0))
    overall = float((I * J) ** 0.5) / 30.0
    values = noise * time_scale[:, None, None] * row_scale[None, :, None] * col_scale[None, None, :]
    return (values * overall).astype(jnp.float32)


def block_levels(rng, extent, cuts, least, high):
    factor_of = 1.0
    for position, shards_of in cuts:
        steps = jax.random.uniform(jax.random.fold_in(jax.random.fold_in(rng, 6), position), (shards_of,), jnp.float32, least / len(cuts), high / len(cuts))
        factor_of = factor_of * jnp.repeat(jnp.exp(steps), extent[position] // shards_of).reshape((-1,) + (1,) * (len(extent) - 1 - position))
    return factor_of


def normal_values(own_key, shape, scale, reach, shards=(), kind=jnp.bfloat16):
    loudness = block_levels(own_key, shape, shards, -0.22, 0.18) if shards else 1.0
    entries = jax.random.normal(own_key, shape, jnp.float32) * scale * loudness
    return jnp.minimum(jnp.maximum(entries, -reach), reach).astype(kind)


def setup_inputs(seed: int = 0) -> dict:
    seeds = jax.random.split(jax.random.key(seed), 4)
    return {
        "tensor": draw_tensor(jax.random.fold_in(seeds[3], 71), 0),
        "second_init": normal_values(seeds[1], (J, R), 1.0, 6.0, ((0, 16),), jnp.float32),
        "third_init": normal_values(seeds[2], (K, R), 1.0, 6.0, (), jnp.float32),
    }


EPSILON = 1e-05
HIGHEST = lax.Precision.HIGHEST

def solve_right(rhs_rows, system):
    cholesky_low = jnp.linalg.cholesky(system)
    halfway = lax.linalg.triangular_solve(cholesky_low, rhs_rows, left_side=False, lower=True, transpose_a=True)
    return lax.linalg.triangular_solve(cholesky_low, halfway, left_side=False, lower=True)

def unit_scale(factor):
    squares = lax.optimization_barrier(jnp.sum(factor * factor, axis=0)) / factor.shape[0]
    return factor / jnp.sqrt(squares + EPSILON)

def gram_local(factor):
    return jnp.dot(factor.T.astype(jnp.float32), factor.astype(jnp.float32), precision=HIGHEST, preferred_element_type=jnp.float32)

def reference(tensor, second_init, third_init):
    second = unit_scale(second_init)
    third = third_init
    gram_second = gram_local(second)
    gram_third = gram_local(third)
    first = None
    for sweep_index in range(ITERS):
        contract_first = lax.dot_general(second.astype(jnp.float32), tensor.astype(jnp.float32), (((0,), (2,)), ((), ())), precision=HIGHEST, preferred_element_type=jnp.float32)
        mttkrp_first = jnp.einsum('rki,kr->ir', contract_first, third, precision=HIGHEST)
        first = unit_scale(solve_right(mttkrp_first, gram_third * gram_second))
        gram_first = gram_local(first)
        contract_second = lax.dot_general(first.astype(jnp.float32), tensor.astype(jnp.float32), (((0,), (1,)), ((), ())), precision=HIGHEST, preferred_element_type=jnp.float32)
        mttkrp_second = jnp.einsum('rkj,kr->jr', contract_second, third, precision=HIGHEST)
        second = unit_scale(solve_right(mttkrp_second, gram_third * gram_first))
        gram_second = gram_local(second)
        mttkrp_third = jnp.einsum('rkj,jr->kr', contract_second, second, precision=HIGHEST)
        third = solve_right(mttkrp_third, gram_first * gram_second)
        gram_third = gram_local(third)
    return (first, second, third)
```

```python
import jax
import jax.numpy as jnp
from jax import lax
from jax.sharding import PartitionSpec as P

ITERS = 5
EPSILON = 1e-05
HIGHEST = lax.Precision.HIGHEST


def matmul(a, b):
    return jnp.dot(a, b, precision=HIGHEST, preferred_element_type=jnp.float32)


def solve_left(system, rhs):
    low = jnp.linalg.cholesky(system)
    half = lax.linalg.triangular_solve(low, rhs, left_side=True, lower=True)
    return lax.linalg.triangular_solve(low, half, left_side=True, lower=True, transpose_a=True)


def gather_sum(x, axis, groups=None):
    n = len(groups[0]) if groups else lax.axis_size(axis)
    copies = jnp.broadcast_to(x, (n,) + x.shape)
    got = lax.all_to_all(copies, axis, 0, 0, axis_index_groups=groups)
    return jnp.sum(got, axis=0)


def pack(gram):
    return jnp.concatenate([gram[:32], gram[32:]], axis=1)


def unpack(packed):
    return jnp.concatenate([packed[:, :64], packed[:, 64:]], axis=0)


def normalise(gram_raw, total):
    diag = jnp.sum(gram_raw * jnp.eye(gram_raw.shape[0], dtype=gram_raw.dtype), axis=1)
    scale = jnp.sqrt(diag / total + EPSILON)
    return scale[:, None], gram_raw / scale[:, None] / scale[None, :]


def per_device(tensor, second_init, third_init):
    n_rows = lax.axis_size("rows")
    total_first = tensor.shape[1] * n_rows
    total_second = tensor.shape[2] * lax.axis_size("cols")
    pairs = [(i, i ^ 1) for i in range(n_rows)]
    chips = [[2 * z + c for z in range(n_rows // 2)] for c in range(2)]

    def sum_rows_big(x):
        x = x + lax.ppermute(x, "rows", pairs)
        return gather_sum(x, "rows", chips)

    second = second_init.T
    third = third_init.T
    gram_third = matmul(third, third.T)
    gram_raw = gather_sum(pack(matmul(second, second.T)), "cols")
    scale_second, gram_second = normalise(unpack(gram_raw), total_second)
    second = second / scale_second
    for _ in range(ITERS):
        weighted = third.T[:, :, None] * second[None]
        part = jnp.sum(
            lax.dot_general(weighted, tensor, (((2,), (2,)), ((0,), (0,))), precision=HIGHEST), axis=0
        )
        first = solve_left(gram_third * gram_second, gather_sum(part, "cols"))
        contract = lax.dot_general(
            jnp.broadcast_to(first, (tensor.shape[0],) + first.shape),
            tensor,
            (((2,), (1,)), ((0,), (0,))),
            precision=HIGHEST,
        )
        part = jnp.sum(contract * third.T[:, :, None], axis=0)
        both = sum_rows_big(jnp.concatenate([part, pack(matmul(first, first.T))], axis=0))
        scale_first, gram_first = normalise(unpack(both[64:]), total_first)
        raw_second = solve_left(gram_third * gram_first, both[:64] / scale_first)
        part = jnp.sum(contract * (raw_second / scale_first)[None], axis=2)
        both = gather_sum(
            jnp.concatenate([part.reshape(16, 128), pack(matmul(raw_second, raw_second.T))], axis=0), "cols"
        )
        scale_second, gram_second = normalise(unpack(both[16:]), total_second)
        whole = gather_sum(both[:16], "rows").reshape(32, 64)
        third = solve_left(gram_first * gram_second, whole.T / scale_second)
        gram_third = matmul(third, third.T)
        second = raw_second / scale_second
    return ((first / scale_first).T, second.T, third.T)


def solution(mesh):
    return jax.shard_map(
        per_device,
        mesh=mesh,
        in_specs=(P(None, "rows", "cols"), P("cols", None), P()),
        out_specs=(P("rows", None), P("cols", None), P()),
        check_vma=False,
    )
```

```python
import jax
import jax.numpy as jnp
from jax import lax
from jax.experimental import pallas as pl
from jax.experimental.pallas import tpu as pltpu
from jax.sharding import PartitionSpec as P

ITERS = 5
EPSILON = 1e-05
HIGHEST = lax.Precision.HIGHEST
PRODUCT = lax.Precision.HIGH


def matmul(a, b):
    return jnp.dot(a, b, precision=HIGHEST, preferred_element_type=jnp.float32)


def inverse_factor(system):
    n = system.shape[0]
    row_id = lax.broadcasted_iota(jnp.int32, (n, n), 0)
    col_id = lax.broadcasted_iota(jnp.int32, (n, n), 1)
    work = jnp.concatenate([system, jnp.where(row_id == col_id, 1.0, 0.0)], axis=1)
    ids = lax.broadcasted_iota(jnp.int32, (n, 1), 0)
    rows = []
    for j in range(n):
        row = work[j : j + 1, :]
        pivot = work[j : j + 1, j : j + 1]
        rows.append(row * lax.rsqrt(pivot))
        if j == n - 1:
            break
        top = (j + 1) // 8 * 8
        below = work[top:]
        column = jnp.where(ids[top:] > j, below[:, j : j + 1], 0.0)
        below = below - column * (row * (1.0 / pivot))
        work = jnp.concatenate([work[:top], below], axis=0) if top else below
    return jnp.concatenate(rows, axis=0)[:, n:]


def invert_kernel(left_ref, right_ref, out_ref):
    low = inverse_factor(left_ref[...] * right_ref[...])
    out_ref[...] = lax.dot_general(
        low, low, (((0,), (0,)), ((), ())), precision=HIGHEST, preferred_element_type=jnp.float32
    )


def inverse_of_product(left, right):
    n = left.shape[0]
    return pl.pallas_call(
        invert_kernel,
        out_shape=jax.ShapeDtypeStruct((n, n), jnp.float32),
        cost_estimate=pl.CostEstimate(flops=2 * n**3, bytes_accessed=12 * n * n, transcendentals=2 * n),
        name="inverse_of_product",
    )(left, right)


def copies(x, n):
    return jnp.broadcast_to(x, (n,) + x.shape)


def pack(gram):
    half = gram.shape[0] // 2
    return jnp.concatenate([gram[:half], gram[half:]], axis=1)


def unpack(packed):
    half = packed.shape[1] // 2
    return jnp.concatenate([packed[:, :half], packed[:, half:]], axis=0)


def normalise(gram_raw, total):
    diag = jnp.sum(gram_raw * jnp.eye(gram_raw.shape[0], dtype=gram_raw.dtype), axis=1)
    scale = jnp.sqrt(diag / total + EPSILON)
    return scale[:, None], gram_raw / scale[:, None] / scale[None, :]


def per_device(tensor, second_init, third_init):
    n_rows = lax.axis_size("rows")
    n_cols = lax.axis_size("cols")
    n_chips = n_rows // 2
    total_first = tensor.shape[1] * n_rows
    total_second = tensor.shape[2] * n_cols
    pairs = [(i, i ^ 1) for i in range(n_rows)]
    chips = [[2 * z + c for z in range(n_chips)] for c in range(2)]
    core = lax.axis_index("rows") % 2

    def sum_cols(x):
        return jnp.sum(lax.all_to_all(copies(x, n_cols), "cols", 0, 0), axis=0)

    def sum_rows_small(x):
        return jnp.sum(lax.all_to_all(copies(x, n_rows), "rows", 0, 0), axis=0)

    def sum_rows(x):
        half = x.shape[0] // 2
        low, high = x[:half], x[half:]
        mine = jnp.where(core == 0, low, high)
        mine = mine + lax.ppermute(jnp.where(core == 0, high, low), "rows", pairs)
        mine = lax.all_to_all(copies(mine, n_chips), "rows", 0, 0, axis_index_groups=chips)
        mine = jnp.sum(mine, axis=0)
        other = lax.ppermute(mine, "rows", pairs)
        return jnp.concatenate([jnp.where(core == 0, mine, other), jnp.where(core == 0, other, mine)], axis=0)

    def first_part(second, third):
        weighted = third.T[:, :, None] * second[None]
        return jnp.sum(
            lax.dot_general(weighted, tensor, (((2,), (2,)), ((0,), (0,))), precision=PRODUCT), axis=0
        )

    raw_second = second_init.T
    third = third_init.T
    gram_third = matmul(third, third.T)
    part = first_part(raw_second, third)
    both = sum_cols(jnp.concatenate([part, pack(matmul(raw_second, raw_second.T))], axis=0))
    scale_second, gram_second = normalise(unpack(both[64:]), total_second)
    inverse = inverse_of_product(gram_third, gram_second)
    summed = both[:64] / scale_second
    for sweep in range(ITERS):
        first = matmul(inverse, summed)
        contract = lax.dot_general(
            jnp.broadcast_to(first, (tensor.shape[0],) + first.shape),
            tensor,
            (((2,), (1,)), ((0,), (0,))),
            precision=PRODUCT,
        )
        part = jnp.sum(contract * third.T[:, :, None], axis=0)
        both = sum_rows(jnp.concatenate([part, pack(matmul(first, first.T))], axis=0))
        scale_first, gram_first = normalise(unpack(both[64:]), total_first)
        inverse = inverse_of_product(gram_third, gram_first)
        raw_second = matmul(inverse, both[:64] / scale_first)
        part = jnp.sum(contract * (raw_second / scale_first)[None], axis=2)
        both = sum_cols(
            jnp.concatenate([part.reshape(16, 128), pack(matmul(raw_second, raw_second.T))], axis=0)
        )
        whole = sum_rows_small(both[:16]).reshape(32, 64)
        scale_second, gram_second = normalise(unpack(both[16:]), total_second)
        inverse = inverse_of_product(gram_first, gram_second)
        third = matmul(inverse, whole.T / scale_second)
        gram_third = matmul(third, third.T)
        second = raw_second / scale_second
        if sweep < ITERS - 1:
            summed = sum_cols(first_part(second, third))
            inverse = inverse_of_product(gram_third, gram_second)
    return ((first / scale_first).T, second.T, third.T)


def solution(mesh):
    return jax.shard_map(
        per_device,
        mesh=mesh,
        in_specs=(P(None, "rows", "cols"), P("cols", None), P()),
        out_specs=(P("rows", None), P("cols", None), P()),
        check_vma=False,
    )
```

```python
import jax
import jax.numpy as jnp
from jax import lax
from jax.experimental import pallas as pl
from jax.experimental.pallas import tpu as pltpu
from jax.sharding import PartitionSpec as P

ITERS = 5
EPSILON = 1e-05
PANEL = 8
HIGHEST = lax.Precision.HIGHEST
PRODUCT = lax.Precision.HIGH
VMEM = pl.BlockSpec(memory_space=pltpu.VMEM)
PARAMS = pltpu.CompilerParams(vmem_limit_bytes=8 * 2**20)


def matmul(a, b, dims=((1,), (0,))):
    return lax.dot_general(a, b, (dims, ((), ())), precision=HIGHEST, preferred_element_type=jnp.float32)


def gram(x):
    return matmul(x, x, ((1,), (1,)))


def identity(n):
    row_id = lax.broadcasted_iota(jnp.int32, (n, n), 0)
    col_id = lax.broadcasted_iota(jnp.int32, (n, n), 1)
    return jnp.where(row_id == col_id, 1.0, 0.0)


def inverse_factor(system):
    n = system.shape[0]
    work = jnp.concatenate([system, identity(n)], axis=1)
    rows = []
    for start in range(0, n, PANEL):
        left = n - start
        ids = lax.broadcasted_iota(jnp.int32, (left, 1), 0)
        columns = [
            jnp.broadcast_to(work[:, start + c : start + c + 1], (left, 2 * n)) for c in range(PANEL)
        ]
        for c in range(PANEL):
            root = lax.rsqrt(columns[c][c : c + 1, :])
            row = work[c : c + 1, :]
            rows.append(row * root)
            if start + c == n - 1:
                break
            factor = jnp.where(ids > c, columns[c] * (root * root), 0.0)
            for d in range(c + 1, PANEL):
                columns[d] = columns[d] - factor * columns[d][c : c + 1, :]
            work = work - factor * row
        if left > PANEL:
            work = work[PANEL:]
    return jnp.concatenate(rows, axis=0)[:, n:]


def inverse(system):
    low = inverse_factor(system)
    return matmul(low, low, ((0,), (0,)))


def pack(gram_raw):
    half = gram_raw.shape[0] // 2
    return jnp.concatenate([gram_raw[:half], gram_raw[half:]], axis=1)


def unpack(packed):
    half = packed.shape[1] // 2
    return jnp.concatenate([packed[:, :half], packed[:, half:]], axis=0)


def normalise(gram_raw, total):
    diag = gram_raw * identity(gram_raw.shape[0])
    scale = jnp.sqrt(jnp.sum(diag, axis=1, keepdims=True) / total + EPSILON)
    across = jnp.sqrt(jnp.sum(diag, axis=0, keepdims=True) / total + EPSILON)
    return scale, gram_raw / scale / across


def invert_kernel(left_ref, right_ref, out_ref):
    out_ref[...] = inverse(left_ref[...] * right_ref[...])


def inverse_of_product(left, right):
    n = left.shape[0]
    return pl.pallas_call(
        invert_kernel,
        out_shape=jax.ShapeDtypeStruct((n, n), jnp.float32),
        in_specs=[VMEM, VMEM],
        out_specs=VMEM,
        cost_estimate=pl.CostEstimate(flops=2 * n**3, bytes_accessed=12 * n * n, transcendentals=2 * n),
        compiler_params=PARAMS,
        name="inverse_of_product",
    )(left, right)


def second_kernel(total, both_ref, third_ref, raw_ref, scaled_ref, packed_ref, gram_ref, scale_ref):
    n = third_ref.shape[0]
    scale, gram_first = normalise(unpack(both_ref[n:, :]), total)
    gram_ref[...] = gram_first
    scale_ref[...] = scale
    raw = matmul(inverse(third_ref[...] * gram_first), both_ref[:n, :] / scale)
    raw_ref[...] = raw
    scaled_ref[...] = raw / scale
    packed_ref[...] = pack(gram(raw))


def solve_second(both, gram_third, total):
    n = gram_third.shape[0]
    wide = both.shape[1]
    shapes = [(n, wide), (n, wide), (n // 2, 2 * n), (n, n), (n, 1)]
    return pl.pallas_call(
        lambda *refs: second_kernel(total, *refs),
        out_shape=[jax.ShapeDtypeStruct(s, jnp.float32) for s in shapes],
        in_specs=[VMEM, VMEM],
        out_specs=[VMEM] * 5,
        cost_estimate=pl.CostEstimate(flops=8 * n**3, bytes_accessed=32 * n * n, transcendentals=4 * n),
        compiler_params=PARAMS,
        name="solve_second",
    )(both, gram_third)


def copies(x, n):
    return jnp.broadcast_to(x, (n,) + x.shape)


def per_device(tensor, second_init, third_init):
    n_rows = lax.axis_size("rows")
    n_cols = lax.axis_size("cols")
    n_chips = n_rows // 2
    total_first = tensor.shape[1] * n_rows
    total_second = tensor.shape[2] * n_cols
    pairs = [(i, i ^ 1) for i in range(n_rows)]
    chips = [[2 * z + c for z in range(n_chips)] for c in range(2)]
    core = lax.axis_index("rows") % 2

    def sum_cols(x):
        return jnp.sum(lax.all_to_all(copies(x, n_cols), "cols", 0, 0), axis=0)

    def sum_rows_small(x):
        return jnp.sum(lax.all_to_all(copies(x, n_rows), "rows", 0, 0), axis=0)

    def sum_rows(x):
        half = x.shape[0] // 2
        low, high = x[:half], x[half:]
        mine = jnp.where(core == 0, low, high)
        mine = mine + lax.ppermute(jnp.where(core == 0, high, low), "rows", pairs)
        mine = lax.all_to_all(copies(mine, n_chips), "rows", 0, 0, axis_index_groups=chips)
        mine = jnp.sum(mine, axis=0)
        other = lax.ppermute(mine, "rows", pairs)
        return jnp.concatenate([jnp.where(core == 0, mine, other), jnp.where(core == 0, other, mine)], axis=0)

    def first_part(second, third):
        weighted = third.T[:, :, None] * second[None]
        return jnp.sum(
            lax.dot_general(weighted, tensor, (((2,), (2,)), ((0,), (0,))), precision=PRODUCT), axis=0
        )

    raw_second = second_init.T
    third = third_init.T
    gram_third = gram(third)
    part = first_part(raw_second, third)
    both = sum_cols(jnp.concatenate([part, pack(gram(raw_second))], axis=0))
    scale_second, gram_second = normalise(unpack(both[64:]), total_second)
    inverted = inverse_of_product(gram_third, gram_second)
    summed = both[:64] / scale_second
    for sweep in range(ITERS):
        first = matmul(inverted, summed)
        contract = lax.dot_general(
            jnp.broadcast_to(first, (tensor.shape[0],) + first.shape),
            tensor,
            (((2,), (1,)), ((0,), (0,))),
            precision=PRODUCT,
        )
        part = jnp.sum(contract * third.T[:, :, None], axis=0)
        both = sum_rows(jnp.concatenate([part, pack(gram(first))], axis=0))
        raw_second, scaled, packed, gram_first, scale_first = solve_second(both, gram_third, total_first)
        part = jnp.sum(contract * scaled[None], axis=2)
        both = sum_cols(jnp.concatenate([part.reshape(16, 128), packed], axis=0))
        whole = sum_rows_small(both[:16]).reshape(32, 64)
        scale_second, gram_second = normalise(unpack(both[16:]), total_second)
        inverted = inverse_of_product(gram_first, gram_second)
        third = matmul(inverted, whole.T / scale_second)
        gram_third = gram(third)
        second = raw_second / scale_second
        if sweep < ITERS - 1:
            summed = sum_cols(first_part(second, third))
            inverted = inverse_of_product(gram_third, gram_second)
    return ((first / scale_first).T, second.T, third.T)


def solution(mesh):
    return jax.shard_map(
        per_device,
        mesh=mesh,
        in_specs=(P(None, "rows", "cols"), P("cols", None), P()),
        out_specs=(P("rows", None), P("cols", None), P()),
        check_vma=False,
    )
```

```python
import jax
import jax.numpy as jnp
from jax import lax
from jax.experimental import pallas as pl
from jax.experimental.pallas import tpu as pltpu
from jax.sharding import PartitionSpec as P

ITERS = 5
EPSILON = 1e-05
PANEL = 8
HIGHEST = lax.Precision.HIGHEST
PRODUCT = lax.Precision.HIGH
VMEM = pl.BlockSpec(memory_space=pltpu.VMEM)
PARAMS = pltpu.CompilerParams(vmem_limit_bytes=8 * 2**20)


def matmul(a, b, dims=((1,), (0,))):
    return lax.dot_general(a, b, (dims, ((), ())), precision=HIGHEST, preferred_element_type=jnp.float32)


def gram(x):
    return matmul(x, x, ((1,), (1,)))


def identity(n):
    row_id = lax.broadcasted_iota(jnp.int32, (n, n), 0)
    col_id = lax.broadcasted_iota(jnp.int32, (n, n), 1)
    return jnp.where(row_id == col_id, 1.0, 0.0)


def inverse_factor(system):
    n = system.shape[0]
    work = jnp.concatenate([system, identity(n)], axis=1)
    rows = []
    for start in range(0, n, PANEL):
        left = n - start
        ids = lax.broadcasted_iota(jnp.int32, (left, 1), 0)
        columns = [
            jnp.broadcast_to(work[:, start + c : start + c + 1], (left, 2 * n)) for c in range(PANEL)
        ]
        for c in range(PANEL):
            root = lax.rsqrt(columns[c][c : c + 1, :])
            row = work[c : c + 1, :]
            rows.append(row * root)
            if start + c == n - 1:
                break
            factor = jnp.where(ids > c, columns[c] * (root * root), 0.0)
            for d in range(c + 1, PANEL):
                columns[d] = columns[d] - factor * columns[d][c : c + 1, :]
            work = work - factor * row
        if left > PANEL:
            work = work[PANEL:]
    return jnp.concatenate(rows, axis=0)[:, n:]


def inverse(system):
    low = inverse_factor(system)
    return matmul(low, low, ((0,), (0,)))


def pack(gram_raw):
    half = gram_raw.shape[0] // 2
    return jnp.concatenate([gram_raw[:half], gram_raw[half:]], axis=1)


def unpack(packed):
    half = packed.shape[1] // 2
    return jnp.concatenate([packed[:, :half], packed[:, half:]], axis=0)


def normalise(gram_raw, total):
    diag = gram_raw * identity(gram_raw.shape[0])
    scale = jnp.sqrt(jnp.sum(diag, axis=1, keepdims=True) / total + EPSILON)
    across = jnp.sqrt(jnp.sum(diag, axis=0, keepdims=True) / total + EPSILON)
    return scale, gram_raw / scale / across


def invert_kernel(left_ref, right_ref, out_ref):
    out_ref[...] = inverse(left_ref[...] * right_ref[...])


def inverse_of_product(left, right):
    n = left.shape[0]
    return pl.pallas_call(
        invert_kernel,
        out_shape=jax.ShapeDtypeStruct((n, n), jnp.float32),
        in_specs=[VMEM, VMEM],
        out_specs=VMEM,
        cost_estimate=pl.CostEstimate(flops=2 * n**3, bytes_accessed=12 * n * n, transcendentals=2 * n),
        compiler_params=PARAMS,
        name="inverse_of_product",
    )(left, right)


def second_kernel(total, both_ref, third_ref, raw_ref, scaled_ref, packed_ref, gram_ref, scale_ref):
    n = third_ref.shape[0]
    scale, gram_first = normalise(unpack(both_ref[n:, :]), total)
    gram_ref[...] = gram_first
    scale_ref[...] = scale
    raw = matmul(inverse(third_ref[...] * gram_first), both_ref[:n, :] / scale)
    raw_ref[...] = raw
    scaled_ref[...] = raw / scale
    packed_ref[...] = pack(gram(raw))


def solve_second(both, gram_third, total):
    n = gram_third.shape[0]
    wide = both.shape[1]
    shapes = [(n, wide), (n, wide), (n // 2, 2 * n), (n, n), (n, 1)]
    return pl.pallas_call(
        lambda *refs: second_kernel(total, *refs),
        out_shape=[jax.ShapeDtypeStruct(s, jnp.float32) for s in shapes],
        in_specs=[VMEM, VMEM],
        out_specs=[VMEM] * 5,
        cost_estimate=pl.CostEstimate(flops=8 * n**3, bytes_accessed=32 * n * n, transcendentals=4 * n),
        compiler_params=PARAMS,
        name="solve_second",
    )(both, gram_third)


def copies(x, n):
    return jnp.broadcast_to(x, (n,) + x.shape)


def per_device(tensor, second_init, third_init):
    n_rows = lax.axis_size("rows")
    total_first = tensor.shape[1] * n_rows
    total_second = tensor.shape[2] * lax.axis_size("cols")
    core = lax.axis_index("rows") % 2

    def swap(x, axis, step):
        return lax.ppermute(x, axis, [(i, i ^ step) for i in range(lax.axis_size(axis))])

    def exchange(x, axis, steps):
        a, b, c = (swap(x, axis, step) for step in steps)
        return (x + a) + (b + c)

    def sum_cols(x):
        return exchange(exchange(x, "cols", (1, 3, 2)), "cols", (4, 12, 8))

    def sum_rows_small(x):
        return jnp.sum(lax.all_to_all(copies(x, n_rows), "rows", 0, 0), axis=0)

    def sum_rows(x):
        half = x.shape[0] // 2
        low, high = x[:half], x[half:]
        mine = jnp.where(core == 0, low, high)
        mine = mine + swap(jnp.where(core == 0, high, low), "rows", 1)
        mine = exchange(mine, "rows", (2, 4, 6))
        mine = mine + swap(mine, "rows", 12)
        other = swap(mine, "rows", 1)
        return jnp.concatenate([jnp.where(core == 0, mine, other), jnp.where(core == 0, other, mine)], axis=0)

    def first_part(second, third):
        weighted = third.T[:, :, None] * second[None]
        return jnp.sum(
            lax.dot_general(weighted, tensor, (((2,), (2,)), ((0,), (0,))), precision=PRODUCT), axis=0
        )

    raw_second = second_init.T
    third = third_init.T
    gram_third = gram(third)
    part = first_part(raw_second, third)
    both = sum_cols(jnp.concatenate([part, pack(gram(raw_second))], axis=0))
    scale_second, gram_second = normalise(unpack(both[64:]), total_second)
    inverted = inverse_of_product(gram_third, gram_second)
    summed = both[:64] / scale_second
    for sweep in range(ITERS):
        first = matmul(inverted, summed)
        contract = lax.dot_general(
            jnp.broadcast_to(first, (tensor.shape[0],) + first.shape),
            tensor,
            (((2,), (1,)), ((0,), (0,))),
            precision=PRODUCT,
        )
        part = jnp.sum(contract * third.T[:, :, None], axis=0)
        both = sum_rows(jnp.concatenate([part, pack(gram(first))], axis=0))
        raw_second, scaled, packed, gram_first, scale_first = solve_second(both, gram_third, total_first)
        part = jnp.sum(contract * scaled[None], axis=2)
        both = sum_cols(jnp.concatenate([part.reshape(16, 128), packed], axis=0))
        whole = sum_rows_small(both[:16]).reshape(32, 64)
        scale_second, gram_second = normalise(unpack(both[16:]), total_second)
        inverted = inverse_of_product(gram_first, gram_second)
        third = matmul(inverted, whole.T / scale_second)
        gram_third = gram(third)
        second = raw_second / scale_second
        if sweep < ITERS - 1:
            summed = sum_cols(first_part(second, third))
            inverted = inverse_of_product(gram_third, gram_second)
    return ((first / scale_first).T, second.T, third.T)


def solution(mesh):
    return jax.shard_map(
        per_device,
        mesh=mesh,
        in_specs=(P(None, "rows", "cols"), P("cols", None), P()),
        out_specs=(P("rows", None), P("cols", None), P()),
        check_vma=False,
    )
```

```python
import jax
import jax.numpy as jnp
from jax import lax
from jax.experimental import pallas as pl
from jax.experimental.pallas import tpu as pltpu
from jax.sharding import PartitionSpec as P

ITERS = 5
EPSILON = 1e-05
PANEL = 8
HIGHEST = lax.Precision.HIGHEST
PRODUCT = lax.Precision.HIGH
VMEM = pl.BlockSpec(memory_space=pltpu.VMEM)
PARAMS = pltpu.CompilerParams(vmem_limit_bytes=8 * 2**20)


def matmul(a, b, dims=((1,), (0,))):
    return lax.dot_general(a, b, (dims, ((), ())), precision=HIGHEST, preferred_element_type=jnp.float32)


def gram(x):
    return matmul(x, x, ((1,), (1,)))


def identity(n):
    row_id = lax.broadcasted_iota(jnp.int32, (n, n), 0)
    col_id = lax.broadcasted_iota(jnp.int32, (n, n), 1)
    return jnp.where(row_id == col_id, 1.0, 0.0)


def inverse_factor(system):
    n = system.shape[0]
    work = jnp.concatenate([system, identity(n)], axis=1)
    rows = []
    for start in range(0, n, PANEL):
        left = n - start
        ids = lax.broadcasted_iota(jnp.int32, (left, 1), 0)
        columns = [
            jnp.broadcast_to(work[:, start + c : start + c + 1], (left, 2 * n)) for c in range(PANEL)
        ]
        for c in range(PANEL):
            root = lax.rsqrt(columns[c][c : c + 1, :])
            row = work[c : c + 1, :]
            rows.append(row * root)
            if start + c == n - 1:
                break
            factor = jnp.where(ids > c, columns[c] * (root * root), 0.0)
            for d in range(c + 1, PANEL):
                columns[d] = columns[d] - factor * columns[d][c : c + 1, :]
            work = work - factor * row
        if left > PANEL:
            work = work[PANEL:]
    return jnp.concatenate(rows, axis=0)[:, n:]


def inverse(system):
    low = inverse_factor(system)
    return matmul(low, low, ((0,), (0,)))


def pack(gram_raw):
    half = gram_raw.shape[0] // 2
    return jnp.concatenate([gram_raw[:half], gram_raw[half:]], axis=1)


def unpack(packed):
    half = packed.shape[1] // 2
    return jnp.concatenate([packed[:, :half], packed[:, half:]], axis=0)


def normalise(gram_raw, total):
    diag = gram_raw * identity(gram_raw.shape[0])
    scale = jnp.sqrt(jnp.sum(diag, axis=1, keepdims=True) / total + EPSILON)
    across = jnp.sqrt(jnp.sum(diag, axis=0, keepdims=True) / total + EPSILON)
    return scale, gram_raw / scale / across


def invert_kernel(left_ref, right_ref, out_ref):
    out_ref[...] = inverse(left_ref[...] * right_ref[...])


def inverse_of_product(left, right):
    n = left.shape[0]
    return pl.pallas_call(
        invert_kernel,
        out_shape=jax.ShapeDtypeStruct((n, n), jnp.float32),
        in_specs=[VMEM, VMEM],
        out_specs=VMEM,
        cost_estimate=pl.CostEstimate(flops=2 * n**3, bytes_accessed=12 * n * n, transcendentals=2 * n),
        compiler_params=PARAMS,
        name="inverse_of_product",
    )(left, right)


def second_kernel(total, both_ref, third_ref, raw_ref, scaled_ref, packed_ref, gram_ref, scale_ref):
    n = third_ref.shape[0]
    scale, gram_first = normalise(unpack(both_ref[n:, :]), total)
    gram_ref[...] = gram_first
    scale_ref[...] = scale
    raw = matmul(inverse(third_ref[...] * gram_first), both_ref[:n, :] / scale)
    raw_ref[...] = raw
    scaled_ref[...] = raw / scale
    packed_ref[...] = pack(gram(raw))


def solve_second(both, gram_third, total):
    n = gram_third.shape[0]
    wide = both.shape[1]
    shapes = [(n, wide), (n, wide), (n // 2, 2 * n), (n, n), (n, 1)]
    return pl.pallas_call(
        lambda *refs: second_kernel(total, *refs),
        out_shape=[jax.ShapeDtypeStruct(s, jnp.float32) for s in shapes],
        in_specs=[VMEM, VMEM],
        out_specs=[VMEM] * 5,
        cost_estimate=pl.CostEstimate(flops=8 * n**3, bytes_accessed=32 * n * n, transcendentals=4 * n),
        compiler_params=PARAMS,
        name="solve_second",
    )(both, gram_third)


def copies(x, n):
    return jnp.broadcast_to(x, (n,) + x.shape)


def per_device(tensor, second_init, third_init):
    n_rows = lax.axis_size("rows")
    total_first = tensor.shape[1] * n_rows
    total_second = tensor.shape[2] * lax.axis_size("cols")
    core = lax.axis_index("rows") % 2

    def swap(x, axis, step):
        return lax.ppermute(x, axis, [(i, i ^ step) for i in range(lax.axis_size(axis))])

    def exchange(x, axis, steps):
        a, b, c = (swap(x, axis, step) for step in steps)
        return (x + a) + (b + c)

    def sum_cols(x):
        return exchange(exchange(x, "cols", (1, 3, 2)), "cols", (4, 12, 8))

    def sum_rows_small(x):
        return jnp.sum(lax.all_to_all(copies(x, n_rows), "rows", 0, 0), axis=0)

    def sum_rows(x):
        half = x.shape[0] // 2
        low, high = x[:half], x[half:]
        mine = jnp.where(core == 0, low, high)
        mine = mine + swap(jnp.where(core == 0, high, low), "rows", 1)
        mine = exchange(mine, "rows", (2, 4, 6))
        mine = mine + swap(mine, "rows", 12)
        other = swap(mine, "rows", 1)
        return jnp.concatenate([jnp.where(core == 0, mine, other), jnp.where(core == 0, other, mine)], axis=0)

    def along(factor, dim):
        return lax.dot_general(
            jnp.broadcast_to(factor, (tensor.shape[0],) + factor.shape),
            tensor,
            (((2,), (dim,)), ((0,), (0,))),
            precision=PRODUCT,
        )

    def weigh(contract, third):
        return jnp.sum(contract * third.T[:, :, None], axis=0)

    raw_second = second_init.T
    third = third_init.T
    gram_third = gram(third)
    part = weigh(along(raw_second, 2), third)
    both = sum_cols(jnp.concatenate([part, pack(gram(raw_second))], axis=0))
    scale_second, gram_second = normalise(unpack(both[64:]), total_second)
    inverted = inverse_of_product(gram_third, gram_second)
    summed = both[:64] / scale_second
    for sweep in range(ITERS):
        first = matmul(inverted, summed)
        contract = along(first, 1)
        part = weigh(contract, third)
        both = sum_rows(jnp.concatenate([part, pack(gram(first))], axis=0))
        raw_second, scaled, packed, gram_first, scale_first = solve_second(both, gram_third, total_first)
        part = jnp.sum(contract * scaled[None], axis=2)
        both = sum_cols(jnp.concatenate([part.reshape(16, 128), packed], axis=0))
        whole = sum_rows_small(both[:16]).reshape(32, 64)
        scale_second, gram_second = normalise(unpack(both[16:]), total_second)
        second = raw_second / scale_second
        ahead = lax.optimization_barrier(along(second, 2))
        inverted = inverse_of_product(gram_first, gram_second)
        third = matmul(inverted, whole.T / scale_second)
        gram_third = gram(third)
        if sweep < ITERS - 1:
            summed = sum_cols(weigh(ahead, third))
            inverted = inverse_of_product(gram_third, gram_second)
    return ((first / scale_first).T, second.T, third.T)


def solution(mesh):
    return jax.shard_map(
        per_device,
        mesh=mesh,
        in_specs=(P(None, "rows", "cols"), P("cols", None), P()),
        out_specs=(P("rows", None), P("cols", None), P()),
        check_vma=False,
    )
```

```python
import jax
import jax.numpy as jnp
from jax import lax
from jax.experimental import pallas as pl
from jax.experimental.pallas import tpu as pltpu
from jax.sharding import PartitionSpec as P

ITERS = 5
EPSILON = 1e-05
PANEL = 16
HIGHEST = lax.Precision.HIGHEST
PRODUCT = lax.Precision.HIGH
VMEM = pl.BlockSpec(memory_space=pltpu.VMEM)
PARAMS = pltpu.CompilerParams(vmem_limit_bytes=8 * 2**20)


def matmul(a, b, dims=((1,), (0,))):
    return lax.dot_general(a, b, (dims, ((), ())), precision=HIGHEST, preferred_element_type=jnp.float32)


def gram(x):
    return matmul(x, x, ((1,), (1,)))


def identity(n):
    row_id = lax.broadcasted_iota(jnp.int32, (n, n), 0)
    col_id = lax.broadcasted_iota(jnp.int32, (n, n), 1)
    return jnp.where(row_id == col_id, 1.0, 0.0)


def inverse_factor(system):
    n = system.shape[0]
    work = jnp.concatenate([system, identity(n)], axis=1)
    rows = []
    for start in range(0, n, PANEL):
        left = n - start
        ids = lax.broadcasted_iota(jnp.int32, (left, 1), 0)
        columns = [
            jnp.broadcast_to(work[:, start + c : start + c + 1], (left, 2 * n)) for c in range(PANEL)
        ]
        for c in range(PANEL):
            root = lax.rsqrt(columns[c][c : c + 1, :])
            row = work[c : c + 1, :]
            rows.append(row * root)
            if start + c == n - 1:
                break
            factor = jnp.where(ids > c, columns[c] * (root * root), 0.0)
            for d in range(c + 1, PANEL):
                columns[d] = columns[d] - factor * columns[d][c : c + 1, :]
            work = work - factor * row
        if left > PANEL:
            work = work[PANEL:]
    return jnp.concatenate(rows, axis=0)[:, n:]


def inverse(system):
    low = inverse_factor(system)
    return matmul(low, low, ((0,), (0,)))


def pack(gram_raw):
    half = gram_raw.shape[0] // 2
    return jnp.concatenate([gram_raw[:half], gram_raw[half:]], axis=1)


def unpack(packed):
    half = packed.shape[1] // 2
    return jnp.concatenate([packed[:, :half], packed[:, half:]], axis=0)


def normalise(gram_raw, total):
    diag = gram_raw * identity(gram_raw.shape[0])
    scale = jnp.sqrt(jnp.sum(diag, axis=1, keepdims=True) / total + EPSILON)
    across = jnp.sqrt(jnp.sum(diag, axis=0, keepdims=True) / total + EPSILON)
    return scale, gram_raw / scale / across


def invert_kernel(left_ref, right_ref, out_ref):
    out_ref[...] = inverse(left_ref[...] * right_ref[...])


def inverse_of_product(left, right):
    n = left.shape[0]
    return pl.pallas_call(
        invert_kernel,
        out_shape=jax.ShapeDtypeStruct((n, n), jnp.float32),
        in_specs=[VMEM, VMEM],
        out_specs=VMEM,
        cost_estimate=pl.CostEstimate(flops=2 * n**3, bytes_accessed=12 * n * n, transcendentals=2 * n),
        compiler_params=PARAMS,
        name="inverse_of_product",
    )(left, right)


def second_kernel(total, both_ref, third_ref, raw_ref, scaled_ref, packed_ref, gram_ref, scale_ref):
    n = third_ref.shape[0]
    scale, gram_first = normalise(unpack(both_ref[n:, :]), total)
    gram_ref[...] = gram_first
    scale_ref[...] = scale
    raw = matmul(inverse(third_ref[...] * gram_first), both_ref[:n, :] / scale)
    raw_ref[...] = raw
    scaled_ref[...] = raw / scale
    packed_ref[...] = pack(gram(raw))


def solve_second(both, gram_third, total):
    n = gram_third.shape[0]
    wide = both.shape[1]
    shapes = [(n, wide), (n, wide), (n // 2, 2 * n), (n, n), (n, 1)]
    return pl.pallas_call(
        lambda *refs: second_kernel(total, *refs),
        out_shape=[jax.ShapeDtypeStruct(s, jnp.float32) for s in shapes],
        in_specs=[VMEM, VMEM],
        out_specs=[VMEM] * 5,
        cost_estimate=pl.CostEstimate(flops=8 * n**3, bytes_accessed=32 * n * n, transcendentals=4 * n),
        compiler_params=PARAMS,
        name="solve_second",
    )(both, gram_third)


def copies(x, n):
    return jnp.broadcast_to(x, (n,) + x.shape)


def per_device(tensor, second_init, third_init):
    n_rows = lax.axis_size("rows")
    total_first = tensor.shape[1] * n_rows
    total_second = tensor.shape[2] * lax.axis_size("cols")
    core = lax.axis_index("rows") % 2

    def swap(x, axis, step):
        return lax.ppermute(x, axis, [(i, i ^ step) for i in range(lax.axis_size(axis))])

    def exchange(x, axis, steps):
        a, b, c = (swap(x, axis, step) for step in steps)
        return (x + a) + (b + c)

    def sum_cols(x):
        return exchange(exchange(x, "cols", (1, 3, 2)), "cols", (4, 12, 8))

    def sum_rows_small(x):
        return jnp.sum(lax.all_to_all(copies(x, n_rows), "rows", 0, 0), axis=0)

    def sum_rows(x):
        half = x.shape[0] // 2
        low, high = x[:half], x[half:]
        mine = jnp.where(core == 0, low, high)
        mine = mine + swap(jnp.where(core == 0, high, low), "rows", 1)
        mine = exchange(mine, "rows", (2, 4, 6))
        mine = mine + swap(mine, "rows", 12)
        other = swap(mine, "rows", 1)
        return jnp.concatenate([jnp.where(core == 0, mine, other), jnp.where(core == 0, other, mine)], axis=0)

    def along(factor, dim):
        return lax.dot_general(
            jnp.broadcast_to(factor, (tensor.shape[0],) + factor.shape),
            tensor,
            (((2,), (dim,)), ((0,), (0,))),
            precision=PRODUCT,
        )

    def weigh(contract, third):
        return jnp.sum(contract * third.T[:, :, None], axis=0)

    raw_second = second_init.T
    third = third_init.T
    gram_third = gram(third)
    part = weigh(along(raw_second, 2), third)
    both = sum_cols(jnp.concatenate([part, pack(gram(raw_second))], axis=0))
    scale_second, gram_second = normalise(unpack(both[64:]), total_second)
    inverted = inverse_of_product(gram_third, gram_second)
    summed = both[:64] / scale_second
    for sweep in range(ITERS):
        first = matmul(inverted, summed)
        contract = along(first, 1)
        part = weigh(contract, third)
        both = sum_rows(jnp.concatenate([part, pack(gram(first))], axis=0))
        raw_second, scaled, packed, gram_first, scale_first = solve_second(both, gram_third, total_first)
        part = jnp.sum(contract * scaled[None], axis=2)
        both = sum_cols(jnp.concatenate([part.reshape(16, 128), packed], axis=0))
        whole = sum_rows_small(both[:16]).reshape(32, 64)
        scale_second, gram_second = normalise(unpack(both[16:]), total_second)
        second = raw_second / scale_second
        ahead = lax.optimization_barrier(along(second, 2))
        inverted = inverse_of_product(gram_first, gram_second)
        third = matmul(inverted, whole.T / scale_second)
        gram_third = gram(third)
        if sweep < ITERS - 1:
            summed = sum_cols(weigh(ahead, third))
            inverted = inverse_of_product(gram_third, gram_second)
    return ((first / scale_first).T, second.T, third.T)


def solution(mesh):
    return jax.shard_map(
        per_device,
        mesh=mesh,
        in_specs=(P(None, "rows", "cols"), P("cols", None), P()),
        out_specs=(P("rows", None), P("cols", None), P()),
        check_vma=False,
    )
```
